32 devices in a mesh: clu: 8 (over z, y), grp: 4 (over x, core).
Axes of the slice: x: 2, y: 2, z: 4, core: 2. Of those that a mesh axis runs over, the one named last changes fastest.
Arguments:
- embeddings: bfloat16 [16384, 768], P(('clu', 'grp')), may hold values from -6 to 6
- cluster_of: int32 [16384], P(('clu', 'grp')), may hold values from 0 to 15, as said below
- new_rows: bfloat16 [512, 768], P(('clu', 'grp')), may hold values from -6 to 6
- centroids: bfloat16 [8192, 768], P(('clu', 'grp')), may hold values from -6 to 6
Outputs:
- dup_score: float32 [16384], P(('clu', 'grp'))
- centroid_score: float32 [512], P(('clu', 'grp'))
The draws below stay inside these ranges and needn't reach their ends.
Inputs may be any that keep to these rules, and one draw needn't show every extreme that they name: `cluster_of`: cluster k is owned by owner k mod 8; among the 512 rows of one device, at most 128 rows belong to the clusters of one owner, and in every such block some owner has exactly 128.
All inputs are finite; a program needn't handle non-finite values.
Results may differ from the reference program's by a relative error of at most 0.0015.
Values may be sent and summed in bfloat16 or wider, within the bound.
A program may use at most 64 MiB of HBM per device.

```python
import jax
import jax.numpy as jnp
from jax import lax

D = 768
TOK_DEV = 512
CPO = 2
CAP = 128
ROWS = 16384
NEW = 512
CENT_DEV = 256
CENTROIDS = 8192
N_CLU = 8
N_GRP = 4


def draw_cluster_of(key, part):
    slot_cap = 2 * TOK_DEV // N_CLU
    slot_total = N_CLU * slot_cap

    def one_block(block_key):
        subkeys = jax.random.split(block_key, 4)
        forced = jax.random.randint(subkeys[0], (), 0, N_CLU)
        shuffled = jax.random.permutation(subkeys[1], slot_total)
        position = jnp.argsort(shuffled).astype(jnp.int32)
        slot_ids = jnp.arange(slot_total, dtype=jnp.int32)
        priority = jnp.where(slot_ids // slot_cap == forced, slot_ids - slot_total, position)
        chosen = jnp.argsort(priority)[:TOK_DEV].astype(jnp.int32)
        owner_ids = chosen // slot_cap
        within = jax.random.randint(subkeys[2], (TOK_DEV,), 0, CPO)
        clusters = owner_ids + N_CLU * within
        return jax.random.permutation(subkeys[3], clusters)
    block_keys = jax.vmap(lambda index_value: jax.random.fold_in(key, index_value))(jnp.arange(N_CLU * N_GRP))
    return jax.vmap(one_block)(block_keys).reshape(-1).astype(jnp.int32)


def shard_levels(own_key, shape, pieces, low, largest):
    def one(dim, shards_of):
        draws = jax.random.uniform(jax.random.fold_in(jax.random.fold_in(own_key, 6), dim), (shards_of,), jnp.float32, low / len(pieces), largest / len(pieces))
        return jnp.repeat(jnp.exp(draws), shape[dim] // shards_of).reshape((-1,) + (1,) * (len(shape) - dim - 1))

    gain = one(*pieces[0])
    for cut in pieces[1:]:
        gain = gain * one(*cut)
    return gain


def gaussian(stream_key, dims, width, most, pieces=(), kind=jnp.bfloat16):
    array = width * jax.random.normal(stream_key, dims, jnp.float32)
    if pieces:
        array = array * shard_levels(stream_key, dims, pieces, -0.22, 0.18)
    return jnp.clip(array, -most, most).astype(kind)


def setup_inputs(seed: int = 0) -> dict:
    key_list = jax.random.split(jax.random.key(seed), 5)
    return {
        "embeddings": gaussian(key_list[0], (ROWS, D), 1.0, 6.0, ((0, 32),)),
        "cluster_of": draw_cluster_of(jax.random.fold_in(key_list[4], 71), 0),
        "new_rows": gaussian(key_list[2], (NEW, D), 1.0, 6.0, ((0, 32),)),
        "centroids": gaussian(key_list[3], (CENTROIDS, D), 1.0, 6.0, ((0, 32),)),
    }


epsilon = 1e-06

def normalize(values):
    wide = values.astype(jnp.float32)
    total = lax.optimization_barrier(jnp.sum(wide * wide, axis=-1, keepdims=True))
    return (wide * lax.rsqrt(total + epsilon)).astype(jnp.bfloat16)

def reference(embeddings, cluster_of, new_rows, centroids):
    normed = normalize(embeddings)
    row_total = normed.shape[0]
    capacity = CAP * N_CLU * N_GRP
    owners = cluster_of % N_CLU
    ordering = jnp.argsort(owners, stable=True).astype(jnp.int32)
    per_owner = lax.optimization_barrier(jnp.sum((owners[None, :] == jnp.arange(N_CLU, dtype=jnp.int32)[:, None]).astype(jnp.int32), axis=1))
    offsets = (jnp.cumsum(per_owner) - per_owner).astype(jnp.int32)
    padded = jnp.concatenate([ordering, jnp.full((capacity,), row_total, jnp.int32)])
    diagonal = jnp.eye(capacity, dtype=bool)

    def one_owner(owner_idx):
        indices = lax.dynamic_slice(padded, (offsets[owner_idx],), (capacity,))
        is_valid = jnp.arange(capacity, dtype=jnp.int32) < per_owner[owner_idx]
        clamped = jnp.minimum(indices, row_total - 1)
        member_units = normed[clamped]
        member_cluster = jnp.where(is_valid, cluster_of[clamped], -1)
        scores = jnp.dot(member_units, member_units.T, preferred_element_type=jnp.float32)
        matched = (member_cluster[:, None] == member_cluster[None, :]) & is_valid[:, None] & jnp.logical_not(diagonal)
        best_match = lax.optimization_barrier(jnp.max(jnp.where(matched, scores, -1.0), axis=1))
        return (jnp.where(is_valid, indices, row_total), best_match)
    target_rows, maxima = lax.map(one_owner, jnp.arange(N_CLU, dtype=jnp.int32))
    dup_score = jnp.zeros((row_total + 1,), jnp.float32).at[target_rows.reshape(-1)].set(maxima.reshape(-1))[:row_total]
    new_unit = normalize(new_rows)
    cent_unit = normalize(centroids).reshape(-1, CENT_DEV, new_rows.shape[1])

    def absorb(running, block_units):
        scores = jnp.dot(new_unit, block_units.T, preferred_element_type=jnp.float32)
        return (jnp.maximum(running, lax.optimization_barrier(jnp.max(scores, axis=1))), None)
    start_value = jnp.full((new_unit.shape[0],), -jnp.inf, jnp.float32)
    centroid_score, unused = lax.scan(absorb, start_value, cent_unit)
    return (dup_score, centroid_score)
```

```python
import functools

import jax
import jax.numpy as jnp
from jax import lax
from jax.experimental import pallas as pl
from jax.experimental.pallas import tpu as pltpu
from jax.sharding import PartitionSpec as P

epsilon = 1e-06
lanes = 128
chunk_order = (0, 1, 6, 7, 2, 3, 4, 5)
chunk_count = len(chunk_order)
stage_count = chunk_count // 2
MESH = pl.DeviceIdType.MESH


def normalize(values):
    wide = values.astype(jnp.float32)
    total = jnp.sum(wide * wide, axis=-1, keepdims=True)
    return (wide * lax.rsqrt(total + epsilon)).astype(jnp.bfloat16)


def pair_scores(left_units, right_units):
    return lax.dot_general(
        left_units, right_units, (((1,), (1,)), ((), ())), preferred_element_type=jnp.float32
    )


def pack_kernel(clu_count, cap, emb_ref, cluster_ref, new_ref, send_ref, ids_ref, slot_ref, unit_ref):
    per_chunk = clu_count // chunk_count
    rows = emb_ref.shape[0]
    slots = clu_count * cap
    me = lax.axis_index("clu")
    unit_ref[...] = normalize(new_ref[...])
    cluster = cluster_ref[...]
    distance = (cluster & (clu_count - 1)) ^ me
    far_chunk = distance // per_chunk
    place = jnp.zeros_like(distance)
    for position, chunk in enumerate(chunk_order):
        place = jnp.where(far_chunk == chunk, position, place)
    place = place * per_chunk + distance % per_chunk
    owner_hot = lax.broadcasted_iota(jnp.int32, (clu_count, rows), 0) == place
    before = lax.broadcasted_iota(jnp.int32, (rows, rows), 0) < lax.broadcasted_iota(
        jnp.int32, (rows, rows), 1
    )
    preceding = jnp.dot(
        owner_hot.astype(jnp.bfloat16),
        before.astype(jnp.bfloat16),
        preferred_element_type=jnp.float32,
    )
    rank = jnp.sum(jnp.where(owner_hot, preceding, 0.0), axis=0, keepdims=True).astype(jnp.int32)
    slot = place * cap + rank
    slot_ref[...] = slot
    chosen = (lax.broadcasted_iota(jnp.int32, (slots, rows), 0) == slot).astype(jnp.bfloat16)
    units = normalize(emb_ref[...])
    send_ref[...] = jnp.dot(chosen, units, preferred_element_type=jnp.float32).astype(jnp.bfloat16)
    marks = jnp.broadcast_to((cluster + 1).astype(jnp.float32), (8, rows)).astype(jnp.bfloat16)
    slot_marks = pair_scores(marks, chosen)
    lane_block = lax.broadcasted_iota(jnp.int32, (8, lanes), 1) // cap
    for block in range(clu_count):
        chunk, inner = divmod(block, per_chunk)
        tile = slot_marks[:, chunk * lanes : (chunk + 1) * lanes]
        ids_ref[block] = jnp.where(lane_block == inner, tile, 0.0)


def exchange_kernel(
    clu_count,
    cap,
    new_count,
    send_ref,
    ids_ref,
    slot_ref,
    new_ref,
    cent_ref,
    dup_ref,
    best_ref,
    held,
    held_ids,
    marks,
    id_rows,
    own_acc,
    mate_acc,
    mate_in,
    new_held,
    cent_unit,
    part,
    part_in,
    message,
    message_in,
    local_sem,
    data_send,
    data_recv,
    id_send,
    id_recv,
    new_send,
    new_recv,
    fwd_send,
    fwd_recv,
    fwd_id_send,
    fwd_id_recv,
    wide_send,
    wide_recv,
    part_send,
    part_recv,
    mate_send,
    mate_recv,
    msg_send,
    msg_recv,
):
    per_chunk = clu_count // chunk_count
    half = lanes
    stage_rows = 2 * half
    me = lax.axis_index("clu")
    grp = lax.axis_index("grp")

    def far(block):
        chunk, inner = divmod(block, per_chunk)
        return {"clu": me ^ (chunk_order[chunk] * per_chunk + inner), "grp": grp}

    def near(step):
        return {"clu": me, "grp": grp ^ step}

    def chunk_row(chunk, kind):
        stage, part_of = divmod(chunk, 2)
        return stage * 3 * stage_rows + kind * stage_rows + part_of * half

    def block_rows(block):
        chunk, inner = divmod(block, per_chunk)
        return pl.ds(chunk_row(chunk, 0) + inner * cap, cap)

    def remote(src, dst, send_sem, recv_sem, device):
        return pltpu.make_async_remote_copy(
            src_ref=src,
            dst_ref=dst,
            send_sem=send_sem,
            recv_sem=recv_sem,
            device_id=device,
            device_id_type=MESH,
        )

    barrier = pltpu.get_barrier_semaphore()
    for block in range(1, clu_count):
        pl.semaphore_signal(barrier, inc=1, device_id=far(block), device_id_type=MESH)
    for step in (1, 2, 3):
        pl.semaphore_signal(barrier, inc=1, device_id=near(step), device_id_type=MESH)

    local = [
        pltpu.make_async_copy(send_ref.at[pl.ds(0, cap)], held.at[block_rows(0)], local_sem.at[0]),
        pltpu.make_async_copy(ids_ref.at[0], held_ids.at[0, 0], local_sem.at[1]),
        pltpu.make_async_copy(new_ref, new_held.at[0, pl.ds(0, new_count)], local_sem.at[2]),
    ]
    for copy in local:
        copy.start()
    pl.semaphore_wait(barrier, clu_count - 1 + 3)

    new_copies = []
    data_copies = [None]
    id_copies = [None]
    for block in range(1, clu_count):
        new_copies.append(
            remote(
                new_ref,
                new_held.at[0, pl.ds(block * new_count, new_count)],
                new_send.at[block],
                new_recv.at[block],
                far(block),
            )
        )
        id_copies.append(
            remote(
                ids_ref.at[block],
                held_ids.at[0, block],
                id_send.at[block],
                id_recv.at[block],
                far(block),
            )
        )
        data_copies.append(
            remote(
                send_ref.at[pl.ds(block * cap, cap)],
                held.at[block_rows(block)],
                data_send.at[block],
                data_recv.at[block],
                far(block),
            )
        )
    for copy in new_copies:
        copy.start()
    for block in range(1, clu_count):
        id_copies[block].start()
        data_copies[block].start()

    own_acc[...] = jnp.full(own_acc.shape, -1.0, jnp.float32)
    mate_acc[...] = jnp.full(mate_acc.shape, -1.0, jnp.float32)
    cent_unit[...] = normalize(cent_ref[...])

    forwards = {}

    def spread_marks(chunk, kind):
        tile = held_ids[kind, chunk * per_chunk]
        for inner in range(1, per_chunk):
            tile = tile + held_ids[kind, chunk * per_chunk + inner]
        square = jnp.concatenate([tile] * (lanes // 8), axis=0)
        marks[pl.ds(chunk_row(chunk, kind), half), :] = jnp.transpose(square)
        if kind < 2:
            stage, part_of = divmod(chunk, 2)
            id_rows[stage, kind, :, pl.ds(part_of * half, half)] = tile

    def pass_on(chunk):
        for inner in range(per_chunk):
            block = chunk * per_chunk + inner
            if block == 0:
                local[0].wait()
                local[1].wait()
            else:
                id_copies[block].wait_recv()
                data_copies[block].wait_recv()
        src_rows = pl.ds(chunk_row(chunk, 0), half)
        src_ids = pl.ds(chunk * per_chunk, per_chunk)
        for kind in (2, 1):
            index = (kind - 1) * chunk_count + chunk
            ids = remote(
                held_ids.at[0, src_ids],
                held_ids.at[kind, src_ids],
                fwd_id_send.at[index],
                fwd_id_recv.at[index],
                near(kind),
            )
            data = remote(
                held.at[src_rows],
                held.at[pl.ds(chunk_row(chunk, kind), half)],
                fwd_send.at[index],
                fwd_recv.at[index],
                near(kind),
            )
            ids.start()
            data.start()
            forwards[chunk, kind] = (ids, data)
        spread_marks(chunk, 0)

    def receive(chunk):
        for kind in (1, 2):
            ids, data = forwards[chunk, kind]
            ids.wait_recv()
            data.wait_recv()
            spread_marks(chunk, kind)

    def fold(scores, matched):
        kept = jnp.where(matched, scores, -1.0)
        return jnp.max(kept.reshape(stage_rows // 8, 8, stage_rows), axis=0)

    def compute(stage):
        receive(2 * stage)
        receive(2 * stage + 1)

        def body(step, carry):
            left = jnp.minimum(step, stage)
            right = jnp.where(step <= stage, stage, step - stage - 1)
            left_base = left * (3 * stage_rows)
            right_base = right * (3 * stage_rows)
            own_cols = held[pl.ds(pl.multiple_of(right_base, stage_rows), stage_rows), :]
            mate_cols = held[
                pl.ds(pl.multiple_of(right_base + stage_rows, stage_rows), stage_rows), :
            ]
            own_ids = id_rows[right, 0][0:1]
            mate_ids = id_rows[right, 1][0:1]
            best = own_acc[right]
            for kind in range(3):
                rows = pl.ds(
                    pl.multiple_of(left_base + kind * stage_rows, stage_rows), stage_rows
                )
                others = held[rows, :]
                mark = marks[rows, :]
                mark = jnp.concatenate([mark, mark], axis=1)
                matched = mark == own_ids
                if kind == 0:
                    row_id = lax.broadcasted_iota(jnp.int32, (stage_rows, stage_rows), 0)
                    col_id = lax.broadcasted_iota(jnp.int32, (stage_rows, stage_rows), 1)
                    shift = (right - left) * stage_rows
                    matched = matched & (row_id - col_id != shift)
                best = jnp.maximum(best, fold(pair_scores(others, own_cols), matched))
                if kind == 2:
                    mate_acc[right] = jnp.maximum(
                        mate_acc[right],
                        fold(pair_scores(others, mate_cols), mark == mate_ids),
                    )
            own_acc[right] = best
            return carry

        lax.fori_loop(0, 2 * stage + 1, body, 0)

    group_rows = clu_count * new_count
    cross_new = remote(
        new_held.at[0], new_held.at[2], wide_send.at[0], wide_recv.at[0], near(2)
    )
    mate_new = remote(new_held.at[0], new_held.at[1], wide_send.at[1], wide_recv.at[1], near(1))
    corner_new = remote(new_held.at[2], new_held.at[3], wide_send.at[2], wide_recv.at[2], near(1))
    part_copies = [
        remote(
            part.at[step],
            part_in.at[step - 1],
            part_send.at[step - 1],
            part_recv.at[step - 1],
            near(step),
        )
        for step in (1, 2, 3)
    ]

    def new_first():
        local[2].wait()
        for copy in new_copies:
            copy.wait_recv()
        cross_new.start()
        mate_new.start()

    def new_second():
        cross_new.wait_recv()
        corner_new.start()

    def new_third():
        mate_new.wait_recv()
        corner_new.wait_recv()
        for step in range(4):
            scores = pair_scores(cent_unit[...], new_held[step])
            top = jnp.max(
                scores.reshape(scores.shape[0] // 8, 8, group_rows), axis=0
            )
            top = jnp.max(top, axis=0, keepdims=True)
            if group_rows == lanes:
                part[step] = jnp.broadcast_to(top, (8, lanes))
            else:
                for row in range(group_rows // lanes):
                    part[step, row : row + 1, :] = top[:, row * lanes : (row + 1) * lanes]
        for copy in part_copies:
            copy.start()

    pass_on(0)
    pass_on(1)
    new_first()
    pass_on(2)
    new_second()
    pass_on(3)
    new_third()
    compute(0)
    pass_on(4)
    pass_on(5)
    compute(1)
    pass_on(6)
    pass_on(7)
    compute(2)
    compute(3)

    mate_copy = remote(mate_acc, mate_in, mate_send.at[0], mate_recv.at[0], near(1))
    mate_copy.start()
    cent_best = part[0]
    for step in (1, 2, 3):
        part_copies[step - 1].wait_recv()
        cent_best = jnp.maximum(cent_best, part_in[step - 1])
    mate_copy.wait_recv()
    for stage in range(stage_count):
        final = jnp.max(
            jnp.maximum(own_acc[stage], mate_in[stage]), axis=0, keepdims=True
        )
        for part_of in range(2):
            message[2 * stage + part_of, 0:8, :] = jnp.broadcast_to(
                final[:, part_of * half : (part_of + 1) * half], (8, lanes)
            )
            message[2 * stage + part_of, 8:, :] = cent_best
    messages = []
    for block in range(1, clu_count):
        copy = remote(
            message.at[block // per_chunk],
            message_in.at[block],
            msg_send.at[block],
            msg_recv.at[block],
            far(block),
        )
        copy.start()
        messages.append(copy)
    message_in[0] = message[0]
    for block in range(1, clu_count):
        new_copies[block - 1].wait_send()
        id_copies[block].wait_send()
        data_copies[block].wait_send()
    for ids, data in forwards.values():
        ids.wait_send()
        data.wait_send()
    for copy in (cross_new, mate_new, corner_new, mate_copy, *part_copies):
        copy.wait_send()
    for copy in messages:
        copy.wait()

    slot = slot_ref[...]
    lane_block = lax.broadcasted_iota(jnp.int32, (1, lanes), 1) // cap
    row_list = []
    for chunk in range(chunk_count):
        row = message_in[chunk * per_chunk, 0:1, :]
        for inner in range(1, per_chunk):
            row = jnp.where(lane_block == inner, message_in[chunk * per_chunk + inner, 0:1, :], row)
        row_list.append(row)
    columns = jnp.transpose(
        jnp.concatenate([jnp.broadcast_to(row, (16, lanes)) for row in row_list], axis=0)
    )
    total = jnp.zeros(slot.shape, jnp.float32)
    position = lax.broadcasted_iota(jnp.int32, (lanes, slot.shape[1]), 0)
    for chunk in range(chunk_count):
        column = columns[:, chunk * 16 : chunk * 16 + 1]
        total = total + jnp.sum(
            jnp.where(position + chunk * lanes == slot, column, 0.0), axis=0, keepdims=True
        )
    dup_ref[...] = total
    best = None
    for block in range(clu_count):
        start = block * new_count
        row = 8 + start // lanes
        piece = message_in[block, row : row + 1, :][:, start % lanes : start % lanes + new_count]
        best = piece if best is None else jnp.maximum(best, piece)
    best_ref[...] = best


def shards(embeddings, cluster_of, new_rows, centroids):
    clu_count = lax.axis_size("clu")
    rows, width = embeddings.shape
    new_count = new_rows.shape[0]
    cap = 2 * rows // clu_count
    slots = clu_count * cap
    assert slots == chunk_count * lanes
    assert lax.axis_size("grp") == 4
    vmem = pl.BlockSpec(memory_space=pltpu.VMEM)
    anywhere = pl.BlockSpec(memory_space=pl.ANY)
    send_units, send_ids, slot, new_unit = pl.pallas_call(
        functools.partial(pack_kernel, clu_count, cap),
        out_shape=(
            jax.ShapeDtypeStruct((slots, width), jnp.bfloat16),
            jax.ShapeDtypeStruct((clu_count, 8, lanes), jnp.float32),
            jax.ShapeDtypeStruct((1, rows), jnp.int32),
            jax.ShapeDtypeStruct((new_count, width), jnp.bfloat16),
        ),
        in_specs=[vmem] * 3,
        out_specs=(vmem,) * 4,
        name="pack",
    )(embeddings, cluster_of.reshape(1, rows), new_rows)
    dma = pltpu.SemaphoreType.DMA
    group_rows = clu_count * new_count
    stage_rows = 2 * lanes
    dup, best = pl.pallas_call(
        functools.partial(exchange_kernel, clu_count, cap, new_count),
        out_shape=(
            jax.ShapeDtypeStruct((1, rows), jnp.float32),
            jax.ShapeDtypeStruct((1, new_count), jnp.float32),
        ),
        in_specs=[anywhere, anywhere, vmem, anywhere, vmem],
        out_specs=(vmem, vmem),
        scratch_shapes=[
            pltpu.VMEM((3 * slots, width), jnp.bfloat16),
            pltpu.VMEM((3, clu_count, 8, lanes), jnp.float32),
            pltpu.VMEM((3 * slots, lanes), jnp.float32),
            pltpu.VMEM((stage_count, 2, 8, stage_rows), jnp.float32),
            pltpu.VMEM((stage_count, 8, stage_rows), jnp.float32),
            pltpu.VMEM((stage_count, 8, stage_rows), jnp.float32),
            pltpu.VMEM((stage_count, 8, stage_rows), jnp.float32),
            pltpu.VMEM((4, group_rows, width), jnp.bfloat16),
            pltpu.VMEM(centroids.shape, jnp.bfloat16),
            pltpu.VMEM((4, 8, lanes), jnp.float32),
            pltpu.VMEM((3, 8, lanes), jnp.float32),
            pltpu.VMEM((chunk_count, 16, lanes), jnp.float32),
            pltpu.VMEM((clu_count, 16, lanes), jnp.float32),
            dma((3,)),
            dma((clu_count,)),
            dma((clu_count,)),
            dma((clu_count,)),
            dma((clu_count,)),
            dma((clu_count,)),
            dma((clu_count,)),
            dma((2 * chunk_count,)),
            dma((2 * chunk_count,)),
            dma((2 * chunk_count,)),
            dma((2 * chunk_count,)),
            dma((3,)),
            dma((3,)),
            dma((3,)),
            dma((3,)),
            dma((1,)),
            dma((1,)),
            dma((clu_count,)),
            dma((clu_count,)),
        ],
        compiler_params=pltpu.CompilerParams(
            collective_id=0, has_side_effects=True, vmem_limit_bytes=48 * 1024 * 1024
        ),
        name="exchange",
    )(send_units, send_ids, slot, new_unit, centroids)
    return (dup.reshape(rows), best.reshape(new_count))


def solution(mesh):
    return jax.shard_map(
        shards,
        mesh=mesh,
        in_specs=(
            P(("clu", "grp"), None),
            P(("clu", "grp")),
            P(("clu", "grp"), None),
            P(("clu", "grp"), None),
        ),
        out_specs=(P(("clu", "grp")), P(("clu", "grp"))),
        check_vma=False,
    )
```

```python
import functools

import jax
import jax.numpy as jnp
from jax import lax
from jax.experimental import pallas as pl
from jax.experimental.pallas import tpu as pltpu
from jax.sharding import PartitionSpec as P

epsilon = 1e-06
lanes = 128
chunk_order = (0, 1, 2, 3, 4, 5, 6, 7)
chunk_count = len(chunk_order)
stage_count = chunk_count // 2
MESH = pl.DeviceIdType.MESH


def normalize(values):
    wide = values.astype(jnp.float32)
    total = jnp.sum(wide * wide, axis=-1, keepdims=True)
    return (wide * lax.rsqrt(total + epsilon)).astype(jnp.bfloat16)


def pair_scores(left_units, right_units):
    return lax.dot_general(
        left_units, right_units, (((1,), (1,)), ((), ())), preferred_element_type=jnp.float32
    )


def exchange_kernel(
    clu_count,
    cap,
    new_count,
    emb_hbm,
    cluster_hbm,
    new_hbm,
    cent_hbm,
    dup_ref,
    best_ref,
    emb_ref,
    cluster_ref,
    new_ref,
    cent_ref,
    units,
    send_ref,
    ids_ref,
    held,
    held_ids,
    marks,
    id_rows,
    own_acc,
    mate_acc,
    mate_in,
    new_held,
    cent_unit,
    part,
    part_in,
    message,
    message_in,
    local_sem,
    data_send,
    data_recv,
    id_send,
    id_recv,
    new_send,
    new_recv,
    fwd_send,
    fwd_recv,
    fwd_id_send,
    fwd_id_recv,
    wide_send,
    wide_recv,
    part_send,
    part_recv,
    mate_send,
    mate_recv,
    msg_send,
    msg_recv,
):
    per_chunk = clu_count // chunk_count
    half = lanes
    stage_rows = 2 * half
    me = lax.axis_index("clu")
    grp = lax.axis_index("grp")

    def far(block):
        chunk, inner = divmod(block, per_chunk)
        return {"clu": me ^ (chunk_order[chunk] * per_chunk + inner), "grp": grp}

    def near(step):
        return {"clu": me, "grp": grp ^ step}

    def chunk_row(chunk, kind):
        stage, part_of = divmod(chunk, 2)
        return stage * 3 * stage_rows + kind * stage_rows + part_of * half

    def block_rows(block):
        chunk, inner = divmod(block, per_chunk)
        return pl.ds(chunk_row(chunk, 0) + inner * cap, cap)

    def remote(src, dst, send_sem, recv_sem, device):
        return pltpu.make_async_remote_copy(
            src_ref=src,
            dst_ref=dst,
            send_sem=send_sem,
            recv_sem=recv_sem,
            device_id=device,
            device_id_type=MESH,
        )

    barrier = pltpu.get_barrier_semaphore()
    for block in range(1, clu_count):
        pl.semaphore_signal(barrier, inc=1, device_id=far(block), device_id_type=MESH)
    for step in (1, 2, 3):
        pl.semaphore_signal(barrier, inc=1, device_id=near(step), device_id_type=MESH)

    local = [
        pltpu.make_async_copy(new_hbm, new_ref, local_sem.at[0]),
        pltpu.make_async_copy(cluster_hbm, cluster_ref, local_sem.at[1]),
        pltpu.make_async_copy(emb_hbm, emb_ref, local_sem.at[2]),
        pltpu.make_async_copy(cent_hbm, cent_ref, local_sem.at[3]),
    ]
    for copy in local:
        copy.start()

    new_copies = []
    data_copies = [None]
    id_copies = [None]
    for block in range(1, clu_count):
        new_copies.append(
            remote(
                new_held.at[0, pl.ds(0, new_count)],
                new_held.at[0, pl.ds(block * new_count, new_count)],
                new_send.at[block],
                new_recv.at[block],
                far(block),
            )
        )
        id_copies.append(
            remote(
                ids_ref.at[block],
                held_ids.at[0, block],
                id_send.at[block],
                id_recv.at[block],
                far(block),
            )
        )
        data_copies.append(
            remote(
                send_ref.at[pl.ds(block * cap, cap)],
                held.at[block_rows(block)],
                data_send.at[block],
                data_recv.at[block],
                far(block),
            )
        )

    local[0].wait()
    new_held[0, 0:new_count, :] = normalize(new_ref[...])
    local[1].wait()
    cluster = cluster_ref[...]
    rows = cluster.shape[1]
    distance = (cluster & (clu_count - 1)) ^ me
    far_chunk = distance // per_chunk
    place = jnp.zeros_like(distance)
    for index, chunk in enumerate(chunk_order):
        place = jnp.where(far_chunk == chunk, index, place)
    place = place * per_chunk + distance % per_chunk
    owner_hot = lax.broadcasted_iota(jnp.int32, (clu_count, rows), 0) == place
    before = lax.broadcasted_iota(jnp.int32, (rows, rows), 0) < lax.broadcasted_iota(
        jnp.int32, (rows, rows), 1
    )
    preceding = jnp.dot(
        owner_hot.astype(jnp.bfloat16),
        before.astype(jnp.bfloat16),
        preferred_element_type=jnp.float32,
    )
    rank = jnp.sum(jnp.where(owner_hot, preceding, 0.0), axis=0, keepdims=True).astype(jnp.int32)
    slot = place * cap + rank
    id_values = jnp.broadcast_to((cluster + 1).astype(jnp.float32), (8, rows)).astype(jnp.bfloat16)
    chunk_slot = lax.broadcasted_iota(jnp.int32, (lanes, rows), 0)
    inner_block = lax.broadcasted_iota(jnp.int32, (8, lanes), 1) // cap
    local[2].wait()
    units[...] = normalize(emb_ref[...])
    pl.semaphore_wait(barrier, clu_count - 1 + 3)
    for copy in new_copies:
        copy.start()

    def pack(chunk):
        chosen = (chunk_slot + chunk * lanes == slot).astype(jnp.bfloat16)
        packed = jnp.dot(chosen, units[...], preferred_element_type=jnp.float32).astype(
            jnp.bfloat16
        )
        tile = pair_scores(id_values, chosen)
        for inner in range(per_chunk):
            block = chunk * per_chunk + inner
            if per_chunk == 1:
                own_tile = tile
            else:
                own_tile = jnp.where(inner_block == inner, tile, 0.0)
            if block == 0:
                held_ids[0, 0] = own_tile
                held[block_rows(0), :] = packed[0:cap]
            else:
                ids_ref[block] = own_tile
        if per_chunk > 1 or chunk > 0:
            send_ref[chunk * lanes : (chunk + 1) * lanes, :] = packed

    def dispatch(chunk):
        for block in range(max(1, chunk * per_chunk), (chunk + 1) * per_chunk):
            id_copies[block].start()
            data_copies[block].start()

    forwards = {}

    def spread_marks(chunk, kind):
        tile = held_ids[kind, chunk * per_chunk]
        for inner in range(1, per_chunk):
            tile = tile + held_ids[kind, chunk * per_chunk + inner]
        square = jnp.concatenate([tile] * (lanes // 8), axis=0)
        marks[pl.ds(chunk_row(chunk, kind), half), :] = jnp.transpose(square)
        if kind < 2:
            stage, part_of = divmod(chunk, 2)
            id_rows[stage, kind, :, pl.ds(part_of * half, half)] = tile

    def pass_on(chunk):
        for inner in range(per_chunk):
            block = chunk * per_chunk + inner
            if block > 0:
                id_copies[block].wait_recv()
                data_copies[block].wait_recv()
        src_rows = pl.ds(chunk_row(chunk, 0), half)
        src_ids = pl.ds(chunk * per_chunk, per_chunk)
        for kind in (2, 1):
            index = (kind - 1) * chunk_count + chunk
            ids = remote(
                held_ids.at[0, src_ids],
                held_ids.at[kind, src_ids],
                fwd_id_send.at[index],
                fwd_id_recv.at[index],
                near(kind),
            )
            data = remote(
                held.at[src_rows],
                held.at[pl.ds(chunk_row(chunk, kind), half)],
                fwd_send.at[index],
                fwd_recv.at[index],
                near(kind),
            )
            ids.start()
            data.start()
            forwards[chunk, kind] = (ids, data)
        spread_marks(chunk, 0)

    def receive(chunk):
        for kind in (1, 2):
            ids, data = forwards[chunk, kind]
            ids.wait_recv()
            data.wait_recv()
            spread_marks(chunk, kind)

    def fold(scores, matched):
        kept = jnp.where(matched, scores, -1.0)
        return jnp.max(kept.reshape(stage_rows // 8, 8, stage_rows), axis=0)

    def tile_rows(stage, kind):
        start = stage * (3 * stage_rows) + kind * stage_rows
        if not isinstance(start, int):
            start = pl.multiple_of(start, stage_rows)
        return pl.ds(start, stage_rows)

    def own_pair(kind, left, right):
        rows = tile_rows(left, kind)
        mark = marks[rows, :]
        matched = jnp.concatenate([mark, mark], axis=1) == id_rows[right, 0][0:1]
        if kind == 0:
            row_id = lax.broadcasted_iota(jnp.int32, (stage_rows, stage_rows), 0)
            col_id = lax.broadcasted_iota(jnp.int32, (stage_rows, stage_rows), 1)
            matched = matched & (row_id - col_id != (right - left) * stage_rows)
        scores = pair_scores(held[rows, :], held[tile_rows(right, 0), :])
        own_acc[right] = jnp.maximum(own_acc[right], fold(scores, matched))

    def mate_pair(left, right):
        rows = tile_rows(left, 2)
        mark = marks[rows, :]
        matched = jnp.concatenate([mark, mark], axis=1) == id_rows[right, 1][0:1]
        scores = pair_scores(held[rows, :], held[tile_rows(right, 1), :])
        mate_acc[right] = jnp.maximum(mate_acc[right], fold(scores, matched))

    def compute(stage):
        receive(2 * stage)
        receive(2 * stage + 1)

        def body(step, carry):
            left = jnp.minimum(step, stage)
            right = jnp.where(step <= stage, stage, step - stage - 1)
            for kind in range(3):
                own_pair(kind, left, right)
            mate_pair(left, right)
            return carry

        lax.fori_loop(0, 2 * stage + 1, body, 0)

    def compute_last():
        last = stage_count - 1

        def own_rows(step, carry):
            own_pair(0, last, step)
            return carry

        def own_cols(step, carry):
            for kind in range(3):
                own_pair(kind, step, last)
            return carry

        def other_rows(step, carry):
            own_pair(1, last, step)
            own_pair(2, last, step)
            mate_pair(last, step)
            return carry

        def mate_cols(step, carry):
            mate_pair(step, last)
            return carry

        lax.fori_loop(0, stage_count, own_rows, 0)
        lax.fori_loop(0, last, own_cols, 0)
        receive(2 * last)
        receive(2 * last + 1)
        lax.fori_loop(0, last, mate_cols, 0)
        lax.fori_loop(0, stage_count, other_rows, 0)

    group_rows = clu_count * new_count
    cross_new = remote(
        new_held.at[0], new_held.at[2], wide_send.at[0], wide_recv.at[0], near(2)
    )
    mate_new = remote(new_held.at[0], new_held.at[1], wide_send.at[1], wide_recv.at[1], near(1))
    corner_new = remote(new_held.at[2], new_held.at[3], wide_send.at[2], wide_recv.at[2], near(1))
    part_copies = [
        remote(
            part.at[step],
            part_in.at[step - 1],
            part_send.at[step - 1],
            part_recv.at[step - 1],
            near(step),
        )
        for step in (1, 2, 3)
    ]

    def new_first():
        for copy in new_copies:
            copy.wait_recv()
        cross_new.start()
        mate_new.start()

    def new_second():
        cross_new.wait_recv()
        corner_new.start()

    def new_third():
        mate_new.wait_recv()
        corner_new.wait_recv()
        for step in range(4):
            scores = pair_scores(cent_unit[...], new_held[step])
            top = jnp.max(
                scores.reshape(scores.shape[0] // 8, 8, group_rows), axis=0
            )
            top = jnp.max(top, axis=0, keepdims=True)
            if group_rows == lanes:
                part[step] = jnp.broadcast_to(top, (8, lanes))
            else:
                for row in range(group_rows // lanes):
                    part[step, row : row + 1, :] = top[:, row * lanes : (row + 1) * lanes]
        for copy in part_copies:
            copy.start()

    pack(0)
    for chunk in range(1, chunk_count):
        pack(chunk)
        if chunk == 1:
            if per_chunk > 1:
                dispatch(0)
        else:
            dispatch(chunk - 1)
    own_acc[...] = jnp.full(own_acc.shape, -1.0, jnp.float32)
    mate_acc[...] = jnp.full(mate_acc.shape, -1.0, jnp.float32)
    dispatch(chunk_count - 1)
    pass_on(0)
    local[3].wait()
    cent_unit[...] = normalize(cent_ref[...])
    pass_on(1)
    new_first()
    pass_on(2)
    pass_on(3)
    new_second()
    compute(0)
    pass_on(4)
    new_third()
    pass_on(5)
    compute(1)
    pass_on(6)
    compute(2)
    pass_on(7)
    compute_last()

    mate_copy = remote(mate_acc, mate_in, mate_send.at[0], mate_recv.at[0], near(1))
    mate_copy.start()
    cent_best = part[0]
    for step in (1, 2, 3):
        part_copies[step - 1].wait_recv()
        cent_best = jnp.maximum(cent_best, part_in[step - 1])
    mate_copy.wait_recv()
    for stage in range(stage_count):
        final = jnp.max(
            jnp.maximum(own_acc[stage], mate_in[stage]), axis=0, keepdims=True
        )
        for part_of in range(2):
            message[2 * stage + part_of, 0:8, :] = jnp.broadcast_to(
                final[:, part_of * half : (part_of + 1) * half], (8, lanes)
            )
            message[2 * stage + part_of, 8:, :] = cent_best
    messages = []
    for block in range(1, clu_count):
        copy = remote(
            message.at[block // per_chunk],
            message_in.at[block],
            msg_send.at[block],
            msg_recv.at[block],
            far(block),
        )
        copy.start()
        messages.append(copy)
    message_in[0] = message[0]
    for block in range(1, clu_count):
        new_copies[block - 1].wait_send()
        id_copies[block].wait_send()
        data_copies[block].wait_send()
    for ids, data in forwards.values():
        ids.wait_send()
        data.wait_send()
    for copy in (cross_new, mate_new, corner_new, mate_copy, *part_copies):
        copy.wait_send()
    for copy in messages:
        copy.wait()

    lane_block = lax.broadcasted_iota(jnp.int32, (1, lanes), 1) // cap
    row_list = []
    for chunk in range(chunk_count):
        row = message_in[chunk * per_chunk, 0:1, :]
        for inner in range(1, per_chunk):
            row = jnp.where(lane_block == inner, message_in[chunk * per_chunk + inner, 0:1, :], row)
        row_list.append(row)
    columns = jnp.transpose(
        jnp.concatenate([jnp.broadcast_to(row, (16, lanes)) for row in row_list], axis=0)
    )
    total = jnp.zeros(slot.shape, jnp.float32)
    position = lax.broadcasted_iota(jnp.int32, (lanes, slot.shape[1]), 0)
    for chunk in range(chunk_count):
        column = columns[:, chunk * 16 : chunk * 16 + 1]
        total = total + jnp.sum(
            jnp.where(position + chunk * lanes == slot, column, 0.0), axis=0, keepdims=True
        )
    dup_ref[...] = total
    best = None
    for block in range(clu_count):
        start = block * new_count
        row = 8 + start // lanes
        piece = message_in[block, row : row + 1, :][:, start % lanes : start % lanes + new_count]
        best = piece if best is None else jnp.maximum(best, piece)
    best_ref[...] = best


def shards(embeddings, cluster_of, new_rows, centroids):
    clu_count = lax.axis_size("clu")
    rows, width = embeddings.shape
    new_count = new_rows.shape[0]
    cap = 2 * rows // clu_count
    slots = clu_count * cap
    assert slots == chunk_count * lanes
    assert lax.axis_size("grp") == 4
    vmem = pl.BlockSpec(memory_space=pltpu.VMEM)
    anywhere = pl.BlockSpec(memory_space=pl.ANY)
    dma = pltpu.SemaphoreType.DMA
    group_rows = clu_count * new_count
    stage_rows = 2 * lanes
    dup, best = pl.pallas_call(
        functools.partial(exchange_kernel, clu_count, cap, new_count),
        out_shape=(
            jax.ShapeDtypeStruct((1, rows), jnp.float32),
            jax.ShapeDtypeStruct((1, new_count), jnp.float32),
        ),
        in_specs=[anywhere] * 4,
        out_specs=(vmem, vmem),
        scratch_shapes=[
            pltpu.VMEM((rows, width), jnp.bfloat16),
            pltpu.VMEM((1, rows), jnp.int32),
            pltpu.VMEM((new_count, width), jnp.bfloat16),
            pltpu.VMEM(centroids.shape, jnp.bfloat16),
            pltpu.VMEM((rows, width), jnp.bfloat16),
            pltpu.VMEM((slots, width), jnp.bfloat16),
            pltpu.VMEM((clu_count, 8, lanes), jnp.float32),
            pltpu.VMEM((3 * slots, width), jnp.bfloat16),
            pltpu.VMEM((3, clu_count, 8, lanes), jnp.float32),
            pltpu.VMEM((3 * slots, lanes), jnp.float32),
            pltpu.VMEM((stage_count, 2, 8, stage_rows), jnp.float32),
            pltpu.VMEM((stage_count, 8, stage_rows), jnp.float32),
            pltpu.VMEM((stage_count, 8, stage_rows), jnp.float32),
            pltpu.VMEM((stage_count, 8, stage_rows), jnp.float32),
            pltpu.VMEM((4, group_rows, width), jnp.bfloat16),
            pltpu.VMEM(centroids.shape, jnp.bfloat16),
            pltpu.VMEM((4, 8, lanes), jnp.float32),
            pltpu.VMEM((3, 8, lanes), jnp.float32),
            pltpu.VMEM((chunk_count, 16, lanes), jnp.float32),
            pltpu.VMEM((clu_count, 16, lanes), jnp.float32),
            dma((4,)),
            dma((clu_count,)),
            dma((clu_count,)),
            dma((clu_count,)),
            dma((clu_count,)),
            dma((clu_count,)),
            dma((clu_count,)),
            dma((2 * chunk_count,)),
            dma((2 * chunk_count,)),
            dma((2 * chunk_count,)),
            dma((2 * chunk_count,)),
            dma((3,)),
            dma((3,)),
            dma((3,)),
            dma((3,)),
            dma((1,)),
            dma((1,)),
            dma((clu_count,)),
            dma((clu_count,)),
        ],
        compiler_params=pltpu.CompilerParams(
            collective_id=0, has_side_effects=True, vmem_limit_bytes=67043328
        ),
        name="exchange",
    )(embeddings, cluster_of.reshape(1, rows), new_rows, centroids)
    return (dup.reshape(rows), best.reshape(new_count))


def solution(mesh):
    return jax.shard_map(
        shards,
        mesh=mesh,
        in_specs=(
            P(("clu", "grp"), None),
            P(("clu", "grp")),
            P(("clu", "grp"), None),
            P(("clu", "grp"), None),
        ),
        out_specs=(P(("clu", "grp")), P(("clu", "grp"))),
        check_vma=False,
    )
```
